256 devices in a mesh: depth: 2 (over core), tile: 128 (over z, y, x).
Axes of the slice: x: 4, y: 4, z: 8, core: 2. Of those that a mesh axis runs over, the one named last changes fastest.
Arguments:
- transmission: float32 [2, 4, 8192, 2048], P(None, 'depth', 'tile'), may hold values from -1 to 1, as said below
- probe: float32 [2, 128, 128], replicated, may hold values from -4 to 4
- scan_rows: int32 [1024], P('tile'), may hold values from 0 to 8064, as said below
- scan_cols: int32 [1024], P('tile'), may hold values from 0 to 1920
- tile_counts: int32 [128], replicated, may hold values from 1 to 8, as said below
- diffraction: float32 [1024, 128, 128], P('tile'), may hold values from 0 to 2
Outputs:
- object_grad: float32 [2, 4, 8192, 2048], P(None, 'depth', 'tile')
- probe_grad: float32 [2, 128, 128], P(None, 'depth')
The draws below stay inside these ranges and needn't reach their ends.
Inputs may be any that keep to these rules, and one draw needn't show every extreme that they name: `scan_rows`: slot i's row lies within [t * 64 - 128/2, t * 64 + 64 - 128/2) for t = i // 8, clipped to the specimen; both ends of the specimen are reached. `tile_counts`: some strip has all 8 slots filled and some strip only one. `transmission`: every entry has magnitude between 0.8 and 1.
All inputs are finite; a program needn't handle non-finite values.
Results may differ from the reference program's by a relative error of at most 0.0003.
Values sent between devices are 32-bit elements; how exact they have to be, the bound alone decides.
No kernel may reach another device: no remote copies, remote signals or barrier semaphores. Data moves between devices by JAX's collectives and lax.ppermute only.
A program may use at most 320 MiB of HBM per device.

```python
import math
import jax
import jax.numpy as jnp
from jax import lax

PROBE = 128
STRIP = 64
COLS = 2048
CAP = 8
SLICES = 4
ROWS = 8192
POSITIONS = 1024


def draw_transmission(key, part):
    key_amp, key_phase = jax.random.split(key)
    shape = (SLICES, ROWS, COLS)
    amplitude = 0.85 + 0.15 * jax.random.uniform(key_amp, shape, jnp.float32)
    phase = jax.random.uniform(key_phase, shape, jnp.float32, -1.5, 1.5)
    return jnp.stack([amplitude * jnp.cos(phase), amplitude * jnp.sin(phase)]).astype(jnp.float32)


def draw_scan_rows(key, part):
    index = jnp.arange(POSITIONS, dtype=jnp.int32)
    strip_of = index // CAP
    tiles = POSITIONS // CAP
    offset = jax.random.randint(key, (POSITIONS,), 0, STRIP, dtype=jnp.int32)
    rows = jnp.clip(strip_of * STRIP - PROBE // 2 + offset, 0, ROWS - PROBE)
    rows = jnp.where(index == 0, 0, rows)
    rows = jnp.where(index == (tiles - 1) * CAP, ROWS - PROBE, rows)
    return rows.astype(jnp.int32)


def draw_tile_counts(key, part):
    tiles = POSITIONS // CAP
    key_a, key_b, key_c = jax.random.split(jax.random.fold_in(key, 7), 3)
    counts = jax.random.randint(key_a, (tiles,), 1, CAP // 2 + 1, dtype=jnp.int32)
    full_tile = jax.random.randint(key_b, (), 0, tiles, dtype=jnp.int32)
    single_tile = (full_tile + jax.random.randint(key_c, (), 1, tiles, dtype=jnp.int32)) % tiles
    index = jnp.arange(tiles, dtype=jnp.int32)
    counts = jnp.where(index == full_tile, CAP, jnp.where(index == single_tile, 1, counts))
    return counts.astype(jnp.int32)


def with_ends(values, rng, least, high):
    longest = values.shape.index(max(values.shape))
    spots = []
    for shift in (0, 1):
        where = [jax.random.randint(jax.random.fold_in(rng, axis), (), 0, length) for axis, length in enumerate(values.shape)]
        where[longest] = (where[longest] + shift) % values.shape[longest]
        spots.append(tuple(where))
    return values.at[spots[0]].set(least).at[spots[1]].set(high)


def block_scale(stream_key, dims, cuts, low, largest):
    loudness = 1.0
    for axis_at, shards_of in cuts:
        steps = jax.random.uniform(jax.random.fold_in(jax.random.fold_in(stream_key, 6), axis_at), (shards_of,), jnp.float32, low / len(cuts), largest / len(cuts))
        loudness = loudness * jnp.repeat(jnp.exp(steps), dims[axis_at] // shards_of).reshape((-1,) + (1,) * (len(dims) - 1 - axis_at))
    return loudness


def centred(stream_key, dims, spread, bound, kind=jnp.bfloat16):
    drawn = jax.random.normal(stream_key, dims, jnp.float32) * spread
    return jnp.minimum(jnp.maximum(drawn, -bound), bound).astype(kind)


def setup_inputs(seed: int = 0) -> dict:
    key_list = jax.random.split(jax.random.key(seed), 7)
    return {
        "transmission": draw_transmission(jax.random.fold_in(key_list[6], 71), 0),
        "probe": centred(key_list[1], (2, PROBE, PROBE), 0.7, 4.0, jnp.float32),
        "scan_rows": draw_scan_rows(jax.random.fold_in(key_list[6], 71), 0),
        "scan_cols": with_ends(jax.random.randint(key_list[3], (POSITIONS,), 0, COLS - PROBE + 1), jax.random.fold_in(key_list[3], 1), 0, COLS - PROBE).astype(jnp.int32),
        "tile_counts": draw_tile_counts(jax.random.fold_in(key_list[6], 71), 0),
        "diffraction": jnp.clip(2.0 * jax.random.uniform(key_list[5], (POSITIONS, PROBE, PROBE), jnp.float32) ** block_scale(key_list[5], (POSITIONS, PROBE, PROBE), ((0, 128),), -0.2, 0.2), 0.0, 2.0),
    }


FRESNEL = 0.5
HIGH = lax.Precision.HIGHEST

def dft_tables(size):
    index = jnp.arange(size, dtype=jnp.int32)
    product = index[:, None] * index[None, :] % size
    angle = 2.0 * math.pi / size * product.astype(jnp.float32)
    scale = 1.0 / math.sqrt(size)
    cosine = jnp.cos(angle) * scale
    sine = jnp.sin(angle) * scale
    freq = ((index + size // 2) % size - size // 2).astype(jnp.float32)
    phase = FRESNEL * math.pi / size * (freq[:, None] ** 2 + freq[None, :] ** 2)
    return (cosine, sine, jnp.cos(phase), jnp.sin(phase))

def left_mul(real_m, imag_m, wave):
    wave_re = wave[..., 0, :, :]
    wave_im = wave[..., 1, :, :]

    def prod(m, x):
        return jnp.einsum('ij,...jk->...ik', m, x, precision=HIGH)
    return jnp.stack([prod(real_m, wave_re) - prod(imag_m, wave_im), prod(real_m, wave_im) + prod(imag_m, wave_re)], axis=-3)

def right_mul(wave, real_m, imag_m):
    wave_re = wave[..., 0, :, :]
    wave_im = wave[..., 1, :, :]

    def prod(x, m):
        return jnp.einsum('...ij,jk->...ik', x, m, precision=HIGH)
    return jnp.stack([prod(wave_re, real_m) - prod(wave_im, imag_m), prod(wave_re, imag_m) + prod(wave_im, real_m)], axis=-3)

def transform(wave, cosine, sine, sign):
    imag_m = sign * sine
    return right_mul(left_mul(cosine, imag_m, wave), cosine, imag_m)

def times(first, second):
    a_re, a_im = (first[..., 0, :, :], first[..., 1, :, :])
    b_re, b_im = (second[..., 0, :, :], second[..., 1, :, :])
    return jnp.stack([a_re * b_re - a_im * b_im, a_re * b_im + a_im * b_re], axis=-3)

def conj_times(first, second):
    a_re, a_im = (first[..., 0, :, :], first[..., 1, :, :])
    b_re, b_im = (second[..., 0, :, :], second[..., 1, :, :])
    return jnp.stack([a_re * b_re + a_im * b_im, a_re * b_im - a_im * b_re], axis=-3)

def propagate(wave, tables, adjoint):
    cosine, sine, kern_cos, kern_sin = tables
    spectrum = transform(wave, cosine, sine, -1.0)
    kernel = jnp.stack([kern_cos, kern_sin if adjoint else -kern_sin])
    return transform(times(kernel, spectrum), cosine, sine, 1.0)

def reference(transmission, probe, scan_rows, scan_cols, tile_counts, diffraction):
    tables = dft_tables(PROBE)
    cosine, sine = (tables[0], tables[1])

    def work(args):
        index, grad, probe_grad = args
        row = scan_rows[index]
        col = scan_cols[index]
        start = (jnp.int32(0), jnp.int32(0), row, col)
        patch = lax.dynamic_slice(transmission, start, (2, SLICES, PROBE, PROBE))
        wave = probe
        inputs = []
        for slice_pos in range(SLICES):
            inputs.append(wave)
            wave = propagate(times(patch[:, slice_pos], wave), tables, False)
        far = transform(wave, cosine, sine, -1.0)
        intensity = far[0] ** 2 + far[1] ** 2
        flow = transform((intensity - diffraction[index])[None] * far, cosine, sine, 1.0)
        pieces = [None] * SLICES
        for slice_pos in reversed(range(SLICES)):
            along = propagate(flow, tables, True)
            pieces[slice_pos] = conj_times(inputs[slice_pos], along)
            flow = conj_times(patch[:, slice_pos], along)
        update = jnp.stack(pieces, axis=1)
        current = lax.dynamic_slice(grad, start, (2, SLICES, PROBE, PROBE))
        grad = lax.dynamic_update_slice(grad, current + update, start)
        return (index, grad, probe_grad + flow)

    def skip(args):
        return args

    def one(index, carry):
        grad, probe_grad = carry
        filled = index % CAP < tile_counts[index // CAP]
        _, grad, probe_grad = lax.cond(filled, work, skip, (index, grad, probe_grad))
        return (grad, probe_grad)
    start_grad = jnp.zeros(transmission.shape, jnp.float32)
    start_probe = jnp.zeros(probe.shape, jnp.float32)
    grad, probe_grad = lax.fori_loop(0, POSITIONS, one, (start_grad, start_probe))
    return (grad, probe_grad)
```

```python
import functools
import math

import jax
import jax.numpy as jnp
import numpy as np
from jax import lax
from jax.experimental import pallas as pl
from jax.experimental.pallas import tpu as pltpu
from jax.sharding import PartitionSpec as P


FRESNEL = 0.5
AXES = ("depth", "tile")
F32 = jnp.float32
BF16 = jnp.bfloat16
GROUPS = 2
VMEM = pl.BlockSpec(memory_space=pltpu.VMEM)
SMEM = pl.BlockSpec(memory_space=pltpu.SMEM)


@functools.lru_cache(None)
def tables(size):
    index = np.arange(size)
    angle = 2.0 * math.pi / size * ((index[:, None] * index[None, :]) % size)
    cosine = np.cos(angle) / math.sqrt(size)
    sine = np.sin(angle) / math.sqrt(size)
    freq = ((index + size // 2) % size - size // 2).astype(np.float64)
    phase = FRESNEL * math.pi / size * (freq[:, None] ** 2 + freq[None, :] ** 2)

    def halves(matrix):
        high = matrix.astype(BF16)
        low = (matrix - high.astype(np.float64)).astype(BF16)
        return high, low

    fwd = np.block([[cosine, -sine], [sine, cosine]])
    inv = np.block([[cosine, sine], [-sine, cosine]])
    fh, fl = halves(fwd)
    ih, il = halves(inv)
    right_f = np.concatenate([fh, fh, fl], axis=0)
    right_i = np.concatenate([ih, ih, il], axis=0)
    left_f = np.concatenate([ih, il, ih], axis=1)
    left_i = np.concatenate([fh, fl, fh], axis=1)
    kern = np.stack([np.cos(phase), np.sin(phase)]).astype(np.float32)
    return right_f, right_i, left_f, left_i, kern


def window_of(col, cols, size):
    block = jnp.minimum(col // size, cols // size - 2)
    return pl.multiple_of(block * size, size), col - block * size


def cut_piece(trans_ref, out_ref, item, col):
    parts, group, strip, cols = trans_ref.shape
    size = out_ref.shape[-1]
    base, shift = window_of(col, cols, size)
    for part in range(parts):
        for s in range(group):
            wide = trans_ref[part, s, :, pl.ds(base, 2 * size)]
            turned = pltpu.roll(wide, lax.rem(2 * size - shift, 2 * size), 1)
            out_ref[item, part, s] = turned[:, :size]


def cut_own_kernel(pos_ref, cols_ref, trans_ref, same_ref, other_ref):
    depth = pos_ref[0]

    @pl.loop(0, same_ref.shape[0])
    def _(item):
        cut_piece(trans_ref, same_ref, item, cols_ref[2 * item + depth])
        cut_piece(trans_ref, other_ref, item, cols_ref[2 * item + 1 - depth])


def cut_halo_kernel(group, pos_ref, up_cols_ref, dn_cols_ref, trans_ref, up_same, up_other, dn_same, dn_other):
    depth = pos_ref[0]
    count = up_same.shape[0]

    @pl.loop(0, count)
    def _(item):
        same = 2 * (group * count + item) + depth
        other = 2 * (group * count + item) + 1 - depth
        cut_piece(trans_ref, up_same, item, up_cols_ref[same])
        cut_piece(trans_ref, up_other, item, up_cols_ref[other])
        cut_piece(trans_ref, dn_same, item, dn_cols_ref[same])
        cut_piece(trans_ref, dn_other, item, dn_cols_ref[other])


def split3(x, axis):
    high = x.astype(BF16)
    low = (x - high.astype(F32)).astype(BF16)
    return high, low


def right_mul(x, table_ref):
    high, low = split3(x, 1)
    return jnp.dot(jnp.concatenate([high, low, high], axis=1), table_ref[...], preferred_element_type=F32)


def left_mul(table_ref, x):
    high, low = split3(x, 0)
    return jnp.dot(table_ref[...], jnp.concatenate([high, high, low], axis=0), preferred_element_type=F32)


def swap(x):
    half = x.shape[0] // 2
    top = jnp.concatenate([x[:half, :half], x[half:, :half]], axis=1)
    bottom = jnp.concatenate([x[:half, half:], x[half:, half:]], axis=1)
    return jnp.concatenate([top, bottom], axis=0)


def compute_kernel(
    group,
    pos_ref,
    rows_ref,
    own_same,
    own_other,
    up_same,
    up_other,
    dn_same,
    dn_other,
    probe_ref,
    diff_ref,
    right_f,
    right_i,
    left_f,
    left_i,
    kern_ref,
    g_own_same,
    g_own_other,
    g_up_same,
    g_up_other,
    g_dn_same,
    g_dn_other,
    p_same,
    p_other,
    stack,
    grads,
    trans,
    waves,
    back,
    probe_sum,
):
    depth, tile, filled = pos_ref[0], pos_ref[1], pos_ref[2]
    pair, parts, per, strip, size = own_same.shape
    slices = 2 * per
    half = size // 2
    mine, theirs = depth * per, (1 - depth) * per
    slots = [2 * (group * pair + item) + depth for item in range(pair)]
    outs = (
        (g_up_same, g_up_other, 0, half),
        (g_own_same, g_own_other, half, strip),
        (g_dn_same, g_dn_other, half + strip, half),
    )

    @pl.when(slots[0] < filled)
    def _work():
        for item in range(pair):
            offset = rows_ref[slots[item]] - (tile * strip - half)
            for part in range(parts):
                for s in range(per):
                    for base, same, other, at, length in (
                        (half - half, up_same, up_other, strip - half, half),
                        (half, own_same, own_other, 0, strip),
                        (half + strip, dn_same, dn_other, 0, half),
                    ):
                        stack[mine + s, pl.ds(base, length), :] = same[item, part, s, at : at + length]
                        stack[theirs + s, pl.ds(base, length), :] = other[item, part, s, at : at + length]
                for s in range(slices):
                    trans[s, part * size : (part + 1) * size, item * size : (item + 1) * size] = stack[
                        s, pl.ds(offset, size), :
                    ]
        live = (slots[1] < filled).astype(F32)
        for part in range(parts):
            rows = slice(part * size, (part + 1) * size)
            waves[0, rows, :size] = probe_ref[part]
            waves[0, rows, size:] = probe_ref[part] * live

        def chain(x, middle):
            x = swap(left_mul(left_f, x))
            x = middle(right_mul(x, right_f))
            x = swap(right_mul(x, right_i))
            return left_mul(left_i, x)

        def kernel_times(sign):
            def middle(x):
                re, im = x[:, :size], x[:, size:]
                kc = jnp.concatenate([kern_ref[0], kern_ref[0]], axis=0)
                ks = jnp.concatenate([kern_ref[1], kern_ref[1]], axis=0)
                if sign > 0:
                    return jnp.concatenate([re * kc - im * ks, im * kc + re * ks], axis=1)
                return jnp.concatenate([re * kc + im * ks, im * kc - re * ks], axis=1)

            return middle

        def residual(x):
            re, im = x[:, :size], x[:, size:]
            measured = jnp.concatenate([diff_ref[slots[0]], diff_ref[slots[1]]], axis=0)
            gap = re * re + im * im - measured
            return jnp.concatenate([gap * re, gap * im], axis=1)

        def forward_times(s):
            t_re, t_im = trans[s, :size], trans[s, size:]
            w_re, w_im = waves[s, :size], waves[s, size:]
            return jnp.concatenate([t_re * w_re - t_im * w_im, t_re * w_im + t_im * w_re], axis=0)

        def adjoint_times(s, along):
            a_re, a_im = along[:size], along[size:]
            w_re, w_im = waves[s, :size], waves[s, size:]
            waves[s, :size] = w_re * a_re + w_im * a_im
            waves[s, size:] = w_re * a_im - w_im * a_re
            t_re, t_im = trans[s, :size], trans[s, size:]
            back[:size] = t_re * a_re + t_im * a_im
            back[size:] = t_re * a_im - t_im * a_re

        @pl.loop(0, slices - 1)
        def _forward(s):
            waves[s + 1] = chain(forward_times(s), kernel_times(-1))

        adjoint_times(slices - 1, chain(forward_times(slices - 1), residual))

        @pl.loop(0, slices - 1)
        def _backward(i):
            adjoint_times(slices - 2 - i, chain(back[...], kernel_times(1)))

        for item in range(pair):
            offset = rows_ref[slots[item]] - (tile * strip - half)
            for part in range(parts):
                grads[...] = jnp.zeros_like(grads)
                for s in range(slices):
                    grads[s, pl.ds(offset, size), :] = waves[
                        s, part * size : (part + 1) * size, item * size : (item + 1) * size
                    ]
                for s in range(per):
                    for same, other, base, length in outs:
                        same[item, part, s] = grads[mine + s, base : base + length]
                        other[item, part, s] = grads[theirs + s, base : base + length]
        for part in range(parts):
            rows = slice(part * size, (part + 1) * size)
            probe_sum[...] = back[rows, :size] + back[rows, size:]
            p_same[part] = probe_sum[pl.ds(depth * half, half)]
            p_other[part] = probe_sum[pl.ds((1 - depth) * half, half)]

    @pl.when(slots[0] >= filled)
    def _rest():
        for same, other, _, _ in outs:
            same[...] = jnp.zeros_like(same)
            other[...] = jnp.zeros_like(other)
        p_same[...] = jnp.zeros_like(p_same)
        p_other[...] = jnp.zeros_like(p_other)


def place_kernel(
    group, start, pos_ref, own_cols, up_cols, dn_cols, own_same, own_other, up_same, up_other, dn_same, dn_other, *rest
):
    out_ref = rest[-1]
    depth = pos_ref[0]
    count, parts, per, strip, size = own_same.shape
    cols = out_ref.shape[-1]
    if start:
        out_ref[...] = jnp.zeros_like(out_ref)
    else:
        out_ref[...] = rest[0][...]

    def add(cols_ref, filled, block_ref, parity):
        @pl.loop(0, count)
        def _(item):
            slot = 2 * (group * count + item) + parity

            @pl.when(slot < filled)
            def _():
                base, shift = window_of(cols_ref[slot], cols, size)
                for part in range(parts):
                    for s in range(per):
                        block = block_ref[item, part, s]
                        wide = jnp.concatenate([block, jnp.zeros_like(block)], axis=1)
                        out_ref[part, s, :, pl.ds(base, 2 * size)] += pltpu.roll(wide, shift, 1)

    add(own_cols, pos_ref[2], own_same, depth)
    add(own_cols, pos_ref[2], own_other, 1 - depth)
    add(up_cols, pos_ref[3], up_same, depth)
    add(up_cols, pos_ref[3], up_other, 1 - depth)
    add(dn_cols, pos_ref[4], dn_same, depth)
    add(dn_cols, pos_ref[4], dn_other, 1 - depth)


def call(kernel, in_specs, out_shapes, args, scratch=(), cost=(1 << 20, 1 << 20), name=None, aliases=None):
    single = not isinstance(out_shapes, (list, tuple))
    return pl.pallas_call(
        kernel,
        out_shape=out_shapes if single else tuple(out_shapes),
        in_specs=in_specs,
        out_specs=VMEM if single else tuple(VMEM for _ in out_shapes),
        scratch_shapes=list(scratch),
        input_output_aliases=aliases or {},
        cost_estimate=pl.CostEstimate(flops=cost[0], bytes_accessed=cost[1], transcendentals=0),
        compiler_params=pltpu.CompilerParams(vmem_limit_bytes=48 << 20),
        name=name,
    )(*args)


def shards(transmission, probe, scan_rows, scan_cols, tile_counts, diffraction):
    parts, per, strip, cols = transmission.shape
    size = probe.shape[-1]
    half = size // 2
    slots = scan_rows.shape[0]
    n_depth, n_tile = lax.axis_size("depth"), lax.axis_size("tile")
    depth, tile = lax.axis_index("depth"), lax.axis_index("tile")
    pair = slots // n_depth // GROUPS
    slices = n_depth * per

    def send(value, cross, by):
        pairs = [
            (d * n_tile + t, (d + cross) % n_depth * n_tile + t + by)
            for d in range(n_depth)
            for t in range(n_tile)
            if 0 <= t + by < n_tile
        ]
        return lax.ppermute(value, AXES, pairs)

    counts = jnp.concatenate([jnp.zeros((1,), jnp.int32), tile_counts, jnp.zeros((1,), jnp.int32)])
    near = lax.dynamic_slice(counts, (tile,), (3,))
    pos = jnp.stack([depth.astype(jnp.int32), tile.astype(jnp.int32), near[1], near[0], near[2]])

    up_cols = send(scan_cols, 0, 1)
    dn_cols = send(scan_cols, 0, -1)
    half_bank = jax.ShapeDtypeStruct((slots // n_depth, parts, per, strip, size), F32)
    pair_bank = jax.ShapeDtypeStruct((pair, parts, per, strip, size), F32)
    own_same, own_cross = call(
        cut_own_kernel,
        [SMEM, SMEM, VMEM],
        [half_bank, half_bank],
        (pos, scan_cols, transmission),
        name="cut_own",
    )
    own_other = send(own_cross, 1, 0)
    halos = []
    for group in range(GROUPS):
        up_s, up_x, dn_s, dn_x = call(
            functools.partial(cut_halo_kernel, group),
            [SMEM, SMEM, SMEM, VMEM],
            [pair_bank] * 4,
            (pos, up_cols, dn_cols, transmission),
            name=f"cut_halo_{group}",
        )
        halos.append((send(dn_s, 0, 1), send(dn_x, 1, 1), send(up_s, 0, -1), send(up_x, 1, -1)))

    right_f, right_i, left_f, left_i, kern = (jnp.asarray(v) for v in tables(size))
    terms, probes = [], []
    for group in range(GROUPS):
        chosen = slice(group * pair, (group + 1) * pair)
        results = call(
            functools.partial(compute_kernel, group),
            [SMEM, SMEM] + [VMEM] * 13,
            [pair_bank] * 6 + [jax.ShapeDtypeStruct((parts, half, size), F32)] * 2,
            (pos, scan_rows, own_same[chosen], own_other[chosen], *halos[group], probe, diffraction)
            + (right_f, right_i, left_f, left_i, kern),
            scratch=[
                pltpu.VMEM((slices, 2 * half + strip, size), F32),
                pltpu.VMEM((slices, 2 * half + strip, size), F32),
                pltpu.VMEM((slices, 2 * size, 2 * size), F32),
                pltpu.VMEM((slices, 2 * size, 2 * size), F32),
                pltpu.VMEM((2 * size, 2 * size), F32),
                pltpu.VMEM((size, size), F32),
            ],
            cost=(3 << 30, 8 << 20),
            name=f"compute_{group}",
        )
        g_own_s, g_own_x, g_up_s, g_up_x, g_dn_s, g_dn_x, p_same, p_other = results
        own_back = send(g_own_x, 1, 0)
        terms.append(
            (g_own_s, own_back, send(g_dn_s, 0, 1), send(g_dn_x, 1, 1), send(g_up_s, 0, -1), send(g_up_x, 1, -1))
        )
        probes.append((p_same, p_other))

    total = probes[0][0] + probes[1][0] + send(probes[0][1] + probes[1][1], 1, 0)
    step = 1
    while step < n_tile:
        pairs = [(d * n_tile + t, d * n_tile + (t ^ step)) for d in range(n_depth) for t in range(n_tile)]
        total = total + lax.ppermute(total, AXES, pairs)
        step *= 2

    grad = None
    grad_shape = jax.ShapeDtypeStruct(transmission.shape, F32)
    for group in range(GROUPS):
        start = grad is None
        grad = call(
            functools.partial(place_kernel, group, start),
            [SMEM] * 4 + [VMEM] * (6 if start else 7),
            grad_shape,
            (pos, scan_cols, up_cols, dn_cols, *terms[group]) + (() if start else (grad,)),
            name=f"place_{group}",
        )
    return (grad, total)


def solution(mesh):
    placed = (P(None, "depth", "tile", None), P(), P("tile"), P("tile"), P(), P("tile", None, None))
    return jax.shard_map(
        shards,
        mesh=mesh,
        in_specs=placed,
        out_specs=(P(None, "depth", "tile", None), P(None, "depth", None)),
        check_vma=False,
    )
```

```python
import functools
import math

import jax
import jax.numpy as jnp
import numpy as np
from jax import lax
from jax.experimental import pallas as pl
from jax.experimental.pallas import tpu as pltpu
from jax.sharding import PartitionSpec as P


FRESNEL = 0.5
AXES = ("depth", "tile")
F32 = jnp.float32
BF16 = jnp.bfloat16
RANK = {1: 0, 2: 1, 4: 2, 8: 3, 16: 4, 32: 5, 64: 6}
VMEM = pl.BlockSpec(memory_space=pltpu.VMEM)
SMEM = pl.BlockSpec(memory_space=pltpu.SMEM)


@functools.lru_cache(None)
def tables(size):
    index = np.arange(size)
    angle = 2.0 * math.pi / size * ((index[:, None] * index[None, :]) % size)
    cosine = np.cos(angle) / math.sqrt(size)
    sine = np.sin(angle) / math.sqrt(size)
    freq = ((index + size // 2) % size - size // 2).astype(np.float64)
    phase = FRESNEL * math.pi / size * (freq[:, None] ** 2 + freq[None, :] ** 2)

    def halves(matrix):
        high = matrix.astype(BF16)
        low = (matrix - high.astype(np.float64)).astype(BF16)
        return high, low

    fwd = np.block([[cosine, -sine], [sine, cosine]])
    inv = np.block([[cosine, sine], [-sine, cosine]])
    kern = np.stack([np.cos(phase), np.sin(phase)]).astype(np.float32)
    return np.stack([*halves(fwd), *halves(inv)]), kern


def window_of(col, cols, size):
    block = jnp.minimum(col // size, cols // size - 2)
    return pl.multiple_of(block * size, size), col - block * size


def cut_piece(trans_ref, out_ref, item, col):
    parts, group, _, cols = trans_ref.shape
    size = out_ref.shape[-1]
    base, shift = window_of(col, cols, size)
    for part in range(parts):
        for s in range(group):
            wide = trans_ref[part, s, :, pl.ds(base, 2 * size)]
            turned = pltpu.roll(wide, lax.rem(2 * size - shift, 2 * size), 1)
            out_ref[item, part, s] = turned[:, :size]


def cut_own_kernel(cols_ref, trans_ref, same_ref, other_ref):
    depth = lax.axis_index("depth")

    @pl.loop(0, same_ref.shape[0])
    def _(item):
        cut_piece(trans_ref, same_ref, item, cols_ref[2 * item + depth])
        cut_piece(trans_ref, other_ref, item, cols_ref[2 * item + 1 - depth])


def cut_halo_kernel(up_cols_ref, dn_cols_ref, trans_ref, up_same, up_other, dn_same, dn_other):
    depth = lax.axis_index("depth")

    @pl.loop(0, up_same.shape[0])
    def _(item):
        same = 2 * item + depth
        other = 2 * item + 1 - depth
        cut_piece(trans_ref, up_same, item, up_cols_ref[same])
        cut_piece(trans_ref, up_other, item, up_cols_ref[other])
        cut_piece(trans_ref, dn_same, item, dn_cols_ref[same])
        cut_piece(trans_ref, dn_other, item, dn_cols_ref[other])


def split3(x):
    high = x.astype(BF16)
    low = (x - high.astype(F32)).astype(BF16)
    return high, low


def right_mul(x, dft_ref, which):
    high, low = split3(x)
    table = jnp.concatenate([dft_ref[which], dft_ref[which], dft_ref[which + 1]], axis=0)
    return jnp.dot(jnp.concatenate([high, low, high], axis=1), table, preferred_element_type=F32)


def left_mul(dft_ref, which, x):
    high, low = split3(x)
    table = jnp.concatenate([dft_ref[which], dft_ref[which + 1], dft_ref[which]], axis=1)
    return jnp.dot(table, jnp.concatenate([high, high, low], axis=0), preferred_element_type=F32)


def swap(x):
    half = x.shape[0] // 2
    top = jnp.concatenate([x[:half, :half], x[half:, :half]], axis=1)
    bottom = jnp.concatenate([x[:half, half:], x[half:, half:]], axis=1)
    return jnp.concatenate([top, bottom], axis=0)


def compute_kernel(
    counts_ref,
    rows_ref,
    own_same,
    own_other,
    up_same,
    up_other,
    dn_same,
    dn_other,
    probe_ref,
    diff_ref,
    dft_ref,
    kern_ref,
    g_own_same,
    g_own_other,
    g_up_same,
    g_up_other,
    g_dn_same,
    g_dn_other,
    p_same,
    p_other,
    stack,
    grads,
    trans,
    waves,
    back,
    probe_sum,
):
    depth, tile = lax.axis_index("depth"), lax.axis_index("tile")
    filled = counts_ref[tile]
    items, parts, per, strip, size = own_same.shape
    pairs = range(items // 2)
    slices = 2 * per
    half = size // 2
    mine, theirs = depth * per, (1 - depth) * per
    slots = [2 * item + depth for item in range(items)]
    outs = (
        (g_up_same, g_up_other, 0, half),
        (g_own_same, g_own_other, half, strip),
        (g_dn_same, g_dn_other, half + strip, half),
    )
    live = [(slot < filled).astype(F32) for slot in slots]
    kc = jnp.concatenate([kern_ref[0], kern_ref[0]], axis=0)
    ks = jnp.concatenate([kern_ref[1], kern_ref[1]], axis=0)

    for item in range(items):
        offset = rows_ref[slots[item]] - (tile * strip - half)
        p, q = item // 2, item % 2
        for part in range(parts):
            for s in range(per):
                for base, same, other, at, length in (
                    (0, up_same, up_other, strip - half, half),
                    (half, own_same, own_other, 0, strip),
                    (half + strip, dn_same, dn_other, 0, half),
                ):
                    stack[mine + s, pl.ds(base, length), :] = same[item, part, s, at : at + length]
                    stack[theirs + s, pl.ds(base, length), :] = other[item, part, s, at : at + length]
            for s in range(slices):
                trans[p, s, part * size : (part + 1) * size, q * size : (q + 1) * size] = stack[
                    s, pl.ds(offset, size), :
                ]
            waves[p, 0, part * size : (part + 1) * size, q * size : (q + 1) * size] = probe_ref[part] * live[item]

    def chain(xs, middle):
        xs = [swap(left_mul(dft_ref, 2, x)) for x in xs]
        xs = [middle(p, right_mul(x, dft_ref, 0)) for p, x in enumerate(xs)]
        xs = [swap(right_mul(x, dft_ref, 2)) for x in xs]
        return [left_mul(dft_ref, 0, x) for x in xs]

    def kernel_times(sign):
        def middle(p, x):
            re, im = x[:, :size], x[:, size:]
            if sign > 0:
                return jnp.concatenate([re * kc - im * ks, im * kc + re * ks], axis=1)
            return jnp.concatenate([re * kc + im * ks, im * kc - re * ks], axis=1)

        return middle

    def residual(p, x):
        re, im = x[:, :size], x[:, size:]
        measured = jnp.concatenate([diff_ref[slots[2 * p]], diff_ref[slots[2 * p + 1]]], axis=0)
        gap = re * re + im * im - measured
        return jnp.concatenate([gap * re, gap * im], axis=1)

    def forward_times(p, s):
        t_re, t_im = trans[p, s, :size], trans[p, s, size:]
        w_re, w_im = waves[p, s, :size], waves[p, s, size:]
        return jnp.concatenate([t_re * w_re - t_im * w_im, t_re * w_im + t_im * w_re], axis=0)

    def adjoint_times(s, alongs):
        for p, along in enumerate(alongs):
            a_re, a_im = along[:size], along[size:]
            w_re, w_im = waves[p, s, :size], waves[p, s, size:]
            waves[p, s, :size] = w_re * a_re + w_im * a_im
            waves[p, s, size:] = w_re * a_im - w_im * a_re
            t_re, t_im = trans[p, s, :size], trans[p, s, size:]
            back[p, :size] = t_re * a_re + t_im * a_im
            back[p, size:] = t_re * a_im - t_im * a_re

    @pl.loop(0, slices - 1)
    def _forward(s):
        for p, x in enumerate(chain([forward_times(p, s) for p in pairs], kernel_times(-1))):
            waves[p, s + 1] = x

    adjoint_times(slices - 1, chain([forward_times(p, slices - 1) for p in pairs], residual))

    @pl.loop(0, slices - 1)
    def _backward(i):
        adjoint_times(slices - 2 - i, chain([back[p] for p in pairs], kernel_times(1)))

    for part in range(parts):
        rows = slice(part * size, (part + 1) * size)
        total = back[0, rows, :size] + back[0, rows, size:]
        for p in pairs[1:]:
            total = total + back[p, rows, :size] + back[p, rows, size:]
        probe_sum[...] = total
        p_same[part] = probe_sum[pl.ds(depth * half, half)]
        p_other[part] = probe_sum[pl.ds((1 - depth) * half, half)]

    for item in range(items):
        offset = rows_ref[slots[item]] - (tile * strip - half)
        p, q = item // 2, item % 2
        for part in range(parts):
            grads[...] = jnp.zeros_like(grads)
            for s in range(slices):
                grads[s, pl.ds(offset, size), :] = waves[
                    p, s, part * size : (part + 1) * size, q * size : (q + 1) * size
                ]
            for s in range(per):
                for same, other, base, length in outs:
                    same[item, part, s] = grads[mine + s, base : base + length]
                    other[item, part, s] = grads[theirs + s, base : base + length]


def add_blocks(out_ref, cols_ref, filled, block_ref, parity):
    count, parts, per, _, size = block_ref.shape
    cols = out_ref.shape[-1]

    @pl.loop(0, count)
    def _(item):
        slot = 2 * item + parity

        @pl.when(slot < filled)
        def _():
            base, shift = window_of(cols_ref[slot], cols, size)
            for part in range(parts):
                for s in range(per):
                    block = block_ref[item, part, s]
                    wide = jnp.concatenate([block, jnp.zeros_like(block)], axis=1)
                    out_ref[part, s, :, pl.ds(base, 2 * size)] += pltpu.roll(wide, shift, 1)


def place_own_kernel(counts_ref, own_cols, own_same, own_other, out_ref):
    depth, tile = lax.axis_index("depth"), lax.axis_index("tile")
    out_ref[...] = jnp.zeros_like(out_ref)
    add_blocks(out_ref, own_cols, counts_ref[tile], own_same, depth)
    add_blocks(out_ref, own_cols, counts_ref[tile], own_other, 1 - depth)


def place_halo_kernel(
    counts_ref, up_cols, dn_cols, up_same, up_other, dn_same, dn_other, so_far, out_ref
):
    depth, tile = lax.axis_index("depth"), lax.axis_index("tile")
    last = counts_ref.shape[0] - 1
    above = jnp.where(tile > 0, counts_ref[jnp.maximum(tile - 1, 0)], 0)
    below = jnp.where(tile < last, counts_ref[jnp.minimum(tile + 1, last)], 0)
    out_ref[...] = so_far[...]
    add_blocks(out_ref, up_cols, above, up_same, depth)
    add_blocks(out_ref, up_cols, above, up_other, 1 - depth)
    add_blocks(out_ref, dn_cols, below, dn_same, depth)
    add_blocks(out_ref, dn_cols, below, dn_other, 1 - depth)


def call(kernel, in_specs, out_shapes, args, scratch=(), cost=(1 << 20, 1 << 20), aliases=None, limit=16):
    single = not isinstance(out_shapes, (list, tuple))
    return pl.pallas_call(
        kernel,
        out_shape=out_shapes if single else tuple(out_shapes),
        in_specs=in_specs,
        out_specs=VMEM if single else tuple(VMEM for _ in out_shapes),
        scratch_shapes=list(scratch),
        input_output_aliases=aliases or {},
        cost_estimate=pl.CostEstimate(flops=cost[0], bytes_accessed=cost[1], transcendentals=0),
        compiler_params=pltpu.CompilerParams(vmem_limit_bytes=limit << 20),
    )(*args)


def work(transmission, probe, scan_rows, scan_cols, tile_counts, diffraction):
    parts, per, strip, _ = transmission.shape
    size = probe.shape[-1]
    half = size // 2
    slots = scan_rows.shape[0]
    n_depth, n_tile = lax.axis_size("depth"), lax.axis_size("tile")
    slices = n_depth * per
    items = slots // n_depth

    def send(value, cross, by):
        pairs = [
            (d * n_tile + t, (d + cross) % n_depth * n_tile + t + by)
            for d in range(n_depth)
            for t in range(n_tile)
            if 0 <= t + by < n_tile
        ]
        return lax.ppermute(value, AXES, pairs)

    up_cols = send(scan_cols, 0, 1)
    dn_cols = send(scan_cols, 0, -1)
    bank = jax.ShapeDtypeStruct((items, parts, per, strip, size), F32)
    own_same, own_cross = call(
        cut_own_kernel, [SMEM, VMEM], [bank, bank], (scan_cols, transmission)
    )
    own_other = send(own_cross, 1, 0)
    up_s, up_x, dn_s, dn_x = call(
        cut_halo_kernel, [SMEM, SMEM, VMEM], [bank] * 4, (up_cols, dn_cols, transmission)
    )
    halos = (send(dn_s, 0, 1), send(dn_x, 1, 1), send(up_s, 0, -1), send(up_x, 1, -1))

    results = call(
        compute_kernel,
        [SMEM, SMEM] + [VMEM] * 10,
        [bank] * 6 + [jax.ShapeDtypeStruct((parts, half, size), F32)] * 2,
        (tile_counts, scan_rows, own_same, own_other, *halos, probe, diffraction)
        + tuple(jnp.asarray(v) for v in tables(size)),
        scratch=[
            pltpu.VMEM((slices, 2 * half + strip, size), F32),
            pltpu.VMEM((slices, 2 * half + strip, size), F32),
            pltpu.VMEM((items // 2, slices, 2 * size, 2 * size), F32),
            pltpu.VMEM((items // 2, slices, 2 * size, 2 * size), F32),
            pltpu.VMEM((items // 2, 2 * size, 2 * size), F32),
            pltpu.VMEM((size, size), F32),
        ],
        cost=(6 << 30, 8 << 20),
        limit=24,
    )
    g_own_s, g_own_x, g_up_s, g_up_x, g_dn_s, g_dn_x, p_same, p_other = results

    total = p_same + send(p_other, 1, 0)
    own_back = send(g_own_x, 1, 0)
    steps = [1 << k for k in range(n_tile.bit_length() - 1)]
    order = sorted(steps, key=lambda step: RANK.get(step, 0))
    for step in order:
        pairs = [(d * n_tile + t, d * n_tile + (t ^ step)) for d in range(n_depth) for t in range(n_tile)]
        total = total + lax.ppermute(total, AXES, pairs)
    up_same = send(g_dn_s, 0, 1)
    up_other = send(g_dn_x, 1, 1)
    dn_same = send(g_up_s, 0, -1)
    dn_other = send(g_up_x, 1, -1)

    grad_shape = jax.ShapeDtypeStruct(transmission.shape, F32)
    grad = call(
        place_own_kernel,
        [SMEM] * 2 + [VMEM] * 2,
        grad_shape,
        (tile_counts, scan_cols, g_own_s, own_back),
    )
    grad = call(
        place_halo_kernel,
        [SMEM] * 3 + [VMEM] * 5,
        grad_shape,
        (tile_counts, up_cols, dn_cols, up_same, up_other, dn_same, dn_other, grad),
    )
    return (grad, total)


def solution(mesh):
    placed = (P(None, "depth", "tile", None), P(), P("tile"), P("tile"), P(), P("tile", None, None))
    return jax.shard_map(
        work,
        mesh=mesh,
        in_specs=placed,
        out_specs=(P(None, "depth", "tile", None), P(None, "depth", None)),
        check_vma=False,
    )
```

```python
import functools
import math

import jax
import jax.numpy as jnp
import numpy as np
from jax import lax
from jax.experimental import pallas as pl
from jax.experimental.pallas import tpu as pltpu
from jax.sharding import PartitionSpec as P


FRESNEL = 0.5
AXES = ("depth", "tile")
F32 = jnp.float32
BF16 = jnp.bfloat16
MASKS = (1, 3, 4, 12, 16, 32, 112)
VMEM = pl.BlockSpec(memory_space=pltpu.VMEM)
SMEM = pl.BlockSpec(memory_space=pltpu.SMEM)


@functools.lru_cache(None)
def tables(size):
    index = np.arange(size)
    angle = 2.0 * math.pi / size * ((index[:, None] * index[None, :]) % size)
    cosine = np.cos(angle) / math.sqrt(size)
    sine = np.sin(angle) / math.sqrt(size)
    freq = ((index + size // 2) % size - size // 2).astype(np.float64)
    phase = FRESNEL * math.pi / size * (freq[:, None] ** 2 + freq[None, :] ** 2)

    def halves(matrix):
        high = matrix.astype(BF16)
        low = (matrix - high.astype(np.float64)).astype(BF16)
        return high, low

    fwd = np.block([[cosine, -sine], [sine, cosine]])
    inv = np.block([[cosine, sine], [-sine, cosine]])
    kern = np.stack([np.cos(phase), np.sin(phase)]).astype(np.float32)
    return np.stack([*halves(fwd), *halves(inv)]), kern


def masks_of(n_tile):
    if n_tile == 1 << len(MASKS):
        return MASKS
    return tuple(1 << k for k in range(n_tile.bit_length() - 1))


def window_of(col, cols, size):
    block = jnp.minimum(col // size, cols // size - 2)
    return pl.multiple_of(block * size, size), col - block * size


def cut_piece(strip_ref, out_ref, item, col, first):
    parts, group, _, cols = strip_ref.shape
    size = out_ref.shape[-1]
    base, shift = window_of(col, cols, size)
    for part in range(parts):
        for s in range(group):
            wide = strip_ref[part, s, :, pl.ds(base, 2 * size)]
            turned = pltpu.roll(wide, lax.rem(2 * size - shift, 2 * size), 1)
            out_ref[item, part, first + s] = turned[:, :size]


def cut_halo_kernel(cols_ref, mine_ref, theirs_ref, pass_ref, keep_ref):
    depth = lax.axis_index("depth")
    group = mine_ref.shape[1]

    @pl.loop(0, keep_ref.shape[0])
    def _(item):
        for out_ref, slot in ((pass_ref, 2 * item + 1 - depth), (keep_ref, 2 * item + depth)):
            cut_piece(mine_ref, out_ref, item, cols_ref[slot], depth * group)
            cut_piece(theirs_ref, out_ref, item, cols_ref[slot], (1 - depth) * group)


def cut_own_kernel(cols_ref, mine_ref, theirs_ref, own_ref):
    depth = lax.axis_index("depth")
    group = mine_ref.shape[1]

    @pl.loop(0, own_ref.shape[0])
    def _(item):
        cut_piece(mine_ref, own_ref, item, cols_ref[2 * item + depth], depth * group)
        cut_piece(theirs_ref, own_ref, item, cols_ref[2 * item + depth], (1 - depth) * group)


def split3(x):
    high = x.astype(BF16)
    low = (x - high.astype(F32)).astype(BF16)
    return high, low


def right_mul(x, dft_ref, which):
    high, low = split3(x)
    table = jnp.concatenate([dft_ref[which], dft_ref[which], dft_ref[which + 1]], axis=0)
    return jnp.dot(jnp.concatenate([high, low, high], axis=1), table, preferred_element_type=F32)


def left_mul(dft_ref, which, x):
    high, low = split3(x)
    table = jnp.concatenate([dft_ref[which], dft_ref[which + 1], dft_ref[which]], axis=1)
    return jnp.dot(table, jnp.concatenate([high, high, low], axis=0), preferred_element_type=F32)


def swap(x):
    half = x.shape[0] // 2
    top = jnp.concatenate([x[:half, :half], x[half:, :half]], axis=1)
    bottom = jnp.concatenate([x[:half, half:], x[half:, half:]], axis=1)
    return jnp.concatenate([top, bottom], axis=0)


def compute_kernel(
    counts_ref,
    rows_ref,
    own,
    halo_keep,
    halo_swap,
    probe_ref,
    diff_ref,
    dft_ref,
    kern_ref,
    g_own,
    g_pass,
    g_keep,
    g_cross,
    p_same,
    p_other,
    stack,
    grads,
    trans,
    waves,
    back,
    probe_sum,
):
    depth, tile = lax.axis_index("depth"), lax.axis_index("tile")
    filled = counts_ref[tile]
    items, parts, slices, strip, size = own.shape
    per = slices // 2
    pairs = range(items // 2)
    half = size // 2
    mine, theirs = depth * per, (1 - depth) * per
    slots = [2 * item + depth for item in range(items)]
    far = half + strip
    from_keep, from_swap = pl.multiple_of(depth * far, half), pl.multiple_of((1 - depth) * far, half)
    to_send, to_cross = from_swap, from_keep
    live = [(slot < filled).astype(F32) for slot in slots]
    kc = jnp.concatenate([kern_ref[0], kern_ref[0]], axis=0)
    ks = jnp.concatenate([kern_ref[1], kern_ref[1]], axis=0)

    for item in range(items):
        offset = rows_ref[slots[item]] - (tile * strip - half)
        p, q = item // 2, item % 2
        for part in range(parts):
            for s in range(slices):
                stack[s, pl.ds(from_keep, half), :] = halo_keep[item, part, s]
                stack[s, half : half + strip, :] = own[item, part, s]
                stack[s, pl.ds(from_swap, half), :] = halo_swap[item, part, s]
            for s in range(slices):
                trans[p, s, part * size : (part + 1) * size, q * size : (q + 1) * size] = stack[
                    s, pl.ds(offset, size), :
                ]
            waves[p, 0, part * size : (part + 1) * size, q * size : (q + 1) * size] = probe_ref[part] * live[item]

    def chain(xs, middle):
        xs = [swap(left_mul(dft_ref, 2, x)) for x in xs]
        xs = [middle(p, right_mul(x, dft_ref, 0)) for p, x in enumerate(xs)]
        xs = [swap(right_mul(x, dft_ref, 2)) for x in xs]
        return [left_mul(dft_ref, 0, x) for x in xs]

    def kernel_times(sign):
        def middle(p, x):
            re, im = x[:, :size], x[:, size:]
            if sign > 0:
                return jnp.concatenate([re * kc - im * ks, im * kc + re * ks], axis=1)
            return jnp.concatenate([re * kc + im * ks, im * kc - re * ks], axis=1)

        return middle

    def residual(p, x):
        re, im = x[:, :size], x[:, size:]
        measured = jnp.concatenate([diff_ref[slots[2 * p]], diff_ref[slots[2 * p + 1]]], axis=0)
        gap = re * re + im * im - measured
        return jnp.concatenate([gap * re, gap * im], axis=1)

    def forward_times(p, s):
        t_re, t_im = trans[p, s, :size], trans[p, s, size:]
        w_re, w_im = waves[p, s, :size], waves[p, s, size:]
        return jnp.concatenate([t_re * w_re - t_im * w_im, t_re * w_im + t_im * w_re], axis=0)

    def adjoint_times(s, alongs):
        for p, along in enumerate(alongs):
            a_re, a_im = along[:size], along[size:]
            w_re, w_im = waves[p, s, :size], waves[p, s, size:]
            waves[p, s, :size] = w_re * a_re + w_im * a_im
            waves[p, s, size:] = w_re * a_im - w_im * a_re
            t_re, t_im = trans[p, s, :size], trans[p, s, size:]
            back[p, :size] = t_re * a_re + t_im * a_im
            back[p, size:] = t_re * a_im - t_im * a_re

    @pl.loop(0, slices - 1)
    def _forward(s):
        for p, x in enumerate(chain([forward_times(p, s) for p in pairs], kernel_times(-1))):
            waves[p, s + 1] = x

    adjoint_times(slices - 1, chain([forward_times(p, slices - 1) for p in pairs], residual))

    @pl.loop(0, slices - 1)
    def _backward(i):
        adjoint_times(slices - 2 - i, chain([back[p] for p in pairs], kernel_times(1)))

    for part in range(parts):
        rows = slice(part * size, (part + 1) * size)
        total = back[0, rows, :size] + back[0, rows, size:]
        for p in pairs[1:]:
            total = total + back[p, rows, :size] + back[p, rows, size:]
        probe_sum[...] = total
        p_same[part] = probe_sum[pl.ds(depth * half, half)]
        p_other[part] = probe_sum[pl.ds((1 - depth) * half, half)]

    for item in range(items):
        offset = rows_ref[slots[item]] - (tile * strip - half)
        p, q = item // 2, item % 2
        for part in range(parts):
            grads[...] = jnp.zeros_like(grads)
            for s in range(slices):
                grads[s, pl.ds(offset, size), :] = waves[
                    p, s, part * size : (part + 1) * size, q * size : (q + 1) * size
                ]
            for s in range(per):
                g_own[item, part, s] = grads[mine + s, half : half + strip]
                g_pass[0, item, part, s] = grads[theirs + s, pl.ds(to_send, half), :]
                g_keep[0, item, part, s] = grads[mine + s, pl.ds(to_send, half), :]
                g_cross[0, item, part, s] = grads[theirs + s, half : half + strip]
                g_cross[1, item, part, s] = grads[mine + s, pl.ds(to_cross, half), :]
                g_cross[2, item, part, s] = grads[theirs + s, pl.ds(to_cross, half), :]


def add_blocks(out_ref, cols_ref, filled, block_ref, parity):
    count, parts, per, _, size = block_ref.shape
    cols = out_ref.shape[-1]

    @pl.loop(0, count)
    def _(item):
        slot = 2 * item + parity

        @pl.when(slot < filled)
        def _():
            base, shift = window_of(cols_ref[slot], cols, size)
            for part in range(parts):
                for s in range(per):
                    block = block_ref[item, part, s]
                    wide = jnp.concatenate([block, jnp.zeros_like(block)], axis=1)
                    out_ref[part, s, :, pl.ds(base, 2 * size)] += pltpu.roll(wide, shift, 1)


def place_own_kernel(counts_ref, own_cols, own_same, crossed, out_ref):
    depth, tile = lax.axis_index("depth"), lax.axis_index("tile")
    out_ref[...] = jnp.zeros_like(out_ref)
    add_blocks(out_ref, own_cols, counts_ref[tile], own_same, depth)
    add_blocks(out_ref, own_cols, counts_ref[tile], crossed.at[0], 1 - depth)


def place_halo_kernel(counts_ref, keep_cols, swap_cols, keep, swap_in, so_far, out_ref):
    depth, tile = lax.axis_index("depth"), lax.axis_index("tile")
    last = counts_ref.shape[0] - 1

    def filled(at):
        return jnp.where((at >= 0) & (at <= last), counts_ref[jnp.clip(at, 0, last)], 0)

    by = 1 - 2 * depth
    out_ref[...] = so_far[...]
    add_blocks(out_ref, keep_cols, filled(tile - by), keep.at[0], depth)
    add_blocks(out_ref, keep_cols, filled(tile - by), keep.at[1], 1 - depth)
    add_blocks(out_ref, swap_cols, filled(tile + by), swap_in.at[0], 1 - depth)
    add_blocks(out_ref, swap_cols, filled(tile + by), swap_in.at[1], depth)


def call(kernel, in_specs, out_shapes, args, scratch=(), cost=(1 << 20, 1 << 20), aliases=None, limit=16):
    single = not isinstance(out_shapes, (list, tuple))
    return pl.pallas_call(
        kernel,
        out_shape=out_shapes if single else tuple(out_shapes),
        in_specs=in_specs,
        out_specs=VMEM if single else tuple(VMEM for _ in out_shapes),
        scratch_shapes=list(scratch),
        input_output_aliases=aliases or {},
        cost_estimate=pl.CostEstimate(flops=cost[0], bytes_accessed=cost[1], transcendentals=0),
        compiler_params=pltpu.CompilerParams(vmem_limit_bytes=limit << 20),
    )(*args)


def work(transmission, probe, scan_rows, scan_cols, tile_counts, diffraction):
    parts, per, strip, _ = transmission.shape
    size = probe.shape[-1]
    half = size // 2
    slots = scan_rows.shape[0]
    n_depth, n_tile = lax.axis_size("depth"), lax.axis_size("tile")
    slices = n_depth * per
    items = slots // n_depth

    swaps = [(d * n_tile + t, (1 - d) * n_tile + t) for d in range(n_depth) for t in range(n_tile)]
    moves = [(t, t + 1) for t in range(n_tile - 1)] + [(n_tile + t + 1, n_tile + t) for t in range(n_tile - 1)]
    asks = [(b, a) for a, b in moves]

    def send(value, pairs):
        return lax.ppermute(value, AXES, pairs)

    swap_cols = send(scan_cols, asks)
    theirs = send(transmission, swaps)
    bank = jax.ShapeDtypeStruct((items, parts, slices, strip, size), F32)
    cut_pass, cut_keep = call(
        cut_halo_kernel, [SMEM, VMEM, VMEM], [bank] * 2, (swap_cols, transmission, theirs)
    )
    passed = send(cut_pass, moves)
    halo_keep = send(cut_keep, moves)
    halo_swap = send(passed, swaps)
    keep_cols = send(swap_cols, swaps)
    own = call(cut_own_kernel, [SMEM, VMEM, VMEM], bank, (scan_cols, transmission, theirs))

    piece = jax.ShapeDtypeStruct((items, parts, per, strip, size), F32)
    both = jax.ShapeDtypeStruct((n_depth, items, parts, per, half, size), F32)
    crossing = jax.ShapeDtypeStruct((3, items, parts, per, half, size), F32)
    results = call(
        compute_kernel,
        [SMEM, SMEM] + [VMEM] * 7,
        [piece, both, both, crossing] + [jax.ShapeDtypeStruct((parts, half, size), F32)] * 2,
        (tile_counts, scan_rows, own, halo_keep, halo_swap, probe, diffraction)
        + tuple(jnp.asarray(v) for v in tables(size)),
        scratch=[
            pltpu.VMEM((slices, 2 * half + strip, size), F32),
            pltpu.VMEM((slices, 2 * half + strip, size), F32),
            pltpu.VMEM((items // 2, slices, 2 * size, 2 * size), F32),
            pltpu.VMEM((items // 2, slices, 2 * size, 2 * size), F32),
            pltpu.VMEM((items // 2, 2 * size, 2 * size), F32),
            pltpu.VMEM((size, size), F32),
        ],
        cost=(6 << 30, 8 << 20),
        limit=24,
    )
    g_own, g_pass, g_keep, g_cross, p_same, p_other = results

    total = p_same + send(p_other, swaps)
    crossed = send(g_cross, swaps)
    for mask in masks_of(n_tile):
        pairs = [(d * n_tile + t, d * n_tile + (t ^ mask)) for d in range(n_depth) for t in range(n_tile)]
        total = total + lax.ppermute(total, AXES, pairs)
    g_pass = lax.dynamic_update_slice(g_pass, crossed[1:2], (1, 0, 0, 0, 0, 0))
    g_keep = lax.dynamic_update_slice(g_keep, crossed[2:3], (1, 0, 0, 0, 0, 0))
    arrived = send(g_pass, moves)
    keep = send(g_keep, moves)
    swap_in = send(arrived, swaps)

    grad_shape = jax.ShapeDtypeStruct(transmission.shape, F32)
    grad = call(
        place_own_kernel,
        [SMEM] * 2 + [VMEM] * 2,
        grad_shape,
        (tile_counts, scan_cols, g_own, crossed),
    )
    grad = call(
        place_halo_kernel,
        [SMEM] * 3 + [VMEM] * 3,
        grad_shape,
        (tile_counts, keep_cols, swap_cols, keep, swap_in, grad),
    )
    return (grad, total)


def solution(mesh):
    placed = (P(None, "depth", "tile", None), P(), P("tile"), P("tile"), P(), P("tile", None, None))
    return jax.shard_map(
        work,
        mesh=mesh,
        in_specs=placed,
        out_specs=(P(None, "depth", "tile", None), P(None, "depth", None)),
        check_vma=False,
    )
```

```python
import functools
import math

import jax
import jax.numpy as jnp
import numpy as np
from jax import lax
from jax.experimental import pallas as pl
from jax.experimental.pallas import tpu as pltpu
from jax.sharding import PartitionSpec as P


FRESNEL = 0.5
AXES = ("depth", "tile")
F32 = jnp.float32
BF16 = jnp.bfloat16
MASKS = (1, 3, 4, 12, 16, 32, 112)
VMEM = pl.BlockSpec(memory_space=pltpu.VMEM)
SMEM = pl.BlockSpec(memory_space=pltpu.SMEM)


@functools.lru_cache(None)
def tables(size):
    index = np.arange(size)
    angle = 2.0 * math.pi / size * ((index[:, None] * index[None, :]) % size)
    cosine = np.cos(angle) / math.sqrt(size)
    sine = np.sin(angle) / math.sqrt(size)
    freq = ((index + size // 2) % size - size // 2).astype(np.float64)
    phase = FRESNEL * math.pi / size * (freq[:, None] ** 2 + freq[None, :] ** 2)

    def halves(matrix):
        high = matrix.astype(BF16)
        low = (matrix - high.astype(np.float64)).astype(BF16)
        return high, low

    fwd = np.block([[cosine, -sine], [sine, cosine]])
    inv = np.block([[cosine, sine], [-sine, cosine]])
    kern = np.stack([np.cos(phase), np.sin(phase)]).astype(np.float32)
    return np.stack([*halves(fwd), *halves(inv)]), kern


def masks_of(n_tile):
    if n_tile == 1 << len(MASKS):
        return MASKS
    return tuple(1 << k for k in range(n_tile.bit_length() - 1))


def window_of(col, cols, size):
    block = jnp.minimum(col // size, cols // size - 2)
    return pl.multiple_of(block * size, size), col - block * size


def cut_piece(strip_ref, out_ref, item, col, first):
    parts, group, _, cols = strip_ref.shape
    size = out_ref.shape[-1]
    base, shift = window_of(col, cols, size)
    for part in range(parts):
        for s in range(group):
            wide = strip_ref[part, s, :, pl.ds(base, 2 * size)]
            turned = pltpu.roll(wide, lax.rem(2 * size - shift, 2 * size), 1)
            out_ref[item, part, first + s] = turned[:, :size]


def cut_kernel(across, cols_ref, mine_ref, theirs_ref, out_ref):
    depth = lax.axis_index("depth")
    group = mine_ref.shape[1]

    @pl.loop(0, out_ref.shape[0])
    def _(item):
        slot = 2 * item + (1 - depth if across else depth)
        cut_piece(mine_ref, out_ref, item, cols_ref[slot], depth * group)
        cut_piece(theirs_ref, out_ref, item, cols_ref[slot], (1 - depth) * group)


def cut_mine_kernel(cols_ref, mine_ref, own_ref):
    depth = lax.axis_index("depth")

    @pl.loop(0, own_ref.shape[0])
    def _(item):
        cut_piece(mine_ref, own_ref, item, cols_ref[2 * item + depth], 0)


def split3(x):
    high = x.astype(BF16)
    low = (x - high.astype(F32)).astype(BF16)
    return high, low


def right_mul(x, dft_ref, which):
    high, low = split3(x)
    table = jnp.concatenate([dft_ref[which], dft_ref[which], dft_ref[which + 1]], axis=0)
    return jnp.dot(jnp.concatenate([high, low, high], axis=1), table, preferred_element_type=F32)


def left_mul(dft_ref, which, x):
    high, low = split3(x)
    table = jnp.concatenate([dft_ref[which], dft_ref[which + 1], dft_ref[which]], axis=1)
    return jnp.dot(table, jnp.concatenate([high, high, low], axis=0), preferred_element_type=F32)


def swap(x):
    half = x.shape[0] // 2
    top = jnp.concatenate([x[:half, :half], x[half:, :half]], axis=1)
    bottom = jnp.concatenate([x[:half, half:], x[half:, half:]], axis=1)
    return jnp.concatenate([top, bottom], axis=0)


def compute_kernel(
    counts_ref,
    rows_ref,
    own_mine,
    own_theirs,
    halo_keep,
    halo_swap,
    probe_ref,
    diff_ref,
    dft_ref,
    kern_ref,
    g_own,
    g_pass,
    g_keep,
    g_cross,
    p_same,
    p_other,
    stack,
    grads,
    trans,
    waves,
    back,
    probe_sum,
):
    depth, tile = lax.axis_index("depth"), lax.axis_index("tile")
    filled = counts_ref[tile]
    items, parts, per, strip, size = own_mine.shape
    slices = 2 * per
    pairs = range(items // 2)
    half = size // 2
    mine, theirs = depth * per, (1 - depth) * per
    slots = [2 * item + depth for item in range(items)]
    far = half + strip
    from_keep, from_swap = pl.multiple_of(depth * far, half), pl.multiple_of((1 - depth) * far, half)
    to_send, to_cross = from_swap, from_keep
    live = [(slot < filled).astype(F32) for slot in slots]
    kc = jnp.concatenate([kern_ref[0], kern_ref[0]], axis=0)
    ks = jnp.concatenate([kern_ref[1], kern_ref[1]], axis=0)

    for item in range(items):
        offset = rows_ref[slots[item]] - (tile * strip - half)
        p, q = item // 2, item % 2
        for part in range(parts):
            for s in range(slices):
                stack[s, pl.ds(from_keep, half), :] = halo_keep[item, part, s]
                stack[s, pl.ds(from_swap, half), :] = halo_swap[item, part, s]
            for s in range(per):
                stack[mine + s, half : half + strip, :] = own_mine[item, part, s]
                stack[theirs + s, half : half + strip, :] = own_theirs[item, part, s]
            for s in range(slices):
                trans[p, s, part * size : (part + 1) * size, q * size : (q + 1) * size] = stack[
                    s, pl.ds(offset, size), :
                ]
            waves[p, 0, part * size : (part + 1) * size, q * size : (q + 1) * size] = probe_ref[part] * live[item]

    def chain(xs, middle):
        xs = [swap(left_mul(dft_ref, 2, x)) for x in xs]
        xs = [middle(p, right_mul(x, dft_ref, 0)) for p, x in enumerate(xs)]
        xs = [swap(right_mul(x, dft_ref, 2)) for x in xs]
        return [left_mul(dft_ref, 0, x) for x in xs]

    def kernel_times(sign):
        def middle(p, x):
            re, im = x[:, :size], x[:, size:]
            if sign > 0:
                return jnp.concatenate([re * kc - im * ks, im * kc + re * ks], axis=1)
            return jnp.concatenate([re * kc + im * ks, im * kc - re * ks], axis=1)

        return middle

    def residual(p, x):
        re, im = x[:, :size], x[:, size:]
        measured = jnp.concatenate([diff_ref[slots[2 * p]], diff_ref[slots[2 * p + 1]]], axis=0)
        gap = re * re + im * im - measured
        return jnp.concatenate([gap * re, gap * im], axis=1)

    def forward_times(p, s):
        t_re, t_im = trans[p, s, :size], trans[p, s, size:]
        w_re, w_im = waves[p, s, :size], waves[p, s, size:]
        return jnp.concatenate([t_re * w_re - t_im * w_im, t_re * w_im + t_im * w_re], axis=0)

    def adjoint_times(s, alongs):
        for p, along in enumerate(alongs):
            a_re, a_im = along[:size], along[size:]
            w_re, w_im = waves[p, s, :size], waves[p, s, size:]
            waves[p, s, :size] = w_re * a_re + w_im * a_im
            waves[p, s, size:] = w_re * a_im - w_im * a_re
            t_re, t_im = trans[p, s, :size], trans[p, s, size:]
            back[p, :size] = t_re * a_re + t_im * a_im
            back[p, size:] = t_re * a_im - t_im * a_re

    @pl.loop(0, slices - 1)
    def _forward(s):
        for p, x in enumerate(chain([forward_times(p, s) for p in pairs], kernel_times(-1))):
            waves[p, s + 1] = x

    adjoint_times(slices - 1, chain([forward_times(p, slices - 1) for p in pairs], residual))

    @pl.loop(0, slices - 1)
    def _backward(i):
        adjoint_times(slices - 2 - i, chain([back[p] for p in pairs], kernel_times(1)))

    for part in range(parts):
        rows = slice(part * size, (part + 1) * size)
        total = back[0, rows, :size] + back[0, rows, size:]
        for p in pairs[1:]:
            total = total + back[p, rows, :size] + back[p, rows, size:]
        probe_sum[...] = total
        p_same[part] = probe_sum[pl.ds(depth * half, half)]
        p_other[part] = probe_sum[pl.ds((1 - depth) * half, half)]

    for item in range(items):
        offset = rows_ref[slots[item]] - (tile * strip - half)
        p, q = item // 2, item % 2
        for part in range(parts):
            grads[...] = jnp.zeros_like(grads)
            for s in range(slices):
                grads[s, pl.ds(offset, size), :] = waves[
                    p, s, part * size : (part + 1) * size, q * size : (q + 1) * size
                ]
            for s in range(per):
                g_own[item, part, s] = grads[mine + s, half : half + strip]
                g_pass[0, item, part, s] = grads[theirs + s, pl.ds(to_send, half), :]
                g_keep[0, item, part, s] = grads[mine + s, pl.ds(to_send, half), :]
                g_cross[0, item, part, s] = grads[theirs + s, half : half + strip]
                g_cross[1, item, part, s] = grads[mine + s, pl.ds(to_cross, half), :]
                g_cross[2, item, part, s] = grads[theirs + s, pl.ds(to_cross, half), :]


def add_blocks(out_ref, cols_ref, filled, block_ref, parity):
    count, parts, per, _, size = block_ref.shape
    cols = out_ref.shape[-1]

    @pl.loop(0, count)
    def _(item):
        slot = 2 * item + parity

        @pl.when(slot < filled)
        def _():
            base, shift = window_of(cols_ref[slot], cols, size)
            for part in range(parts):
                for s in range(per):
                    block = block_ref[item, part, s]
                    wide = jnp.concatenate([block, jnp.zeros_like(block)], axis=1)
                    out_ref[part, s, :, pl.ds(base, 2 * size)] += pltpu.roll(wide, shift, 1)


def place_own_kernel(counts_ref, own_cols, own_same, crossed, out_ref):
    depth, tile = lax.axis_index("depth"), lax.axis_index("tile")
    out_ref[...] = jnp.zeros_like(out_ref)
    add_blocks(out_ref, own_cols, counts_ref[tile], own_same, depth)
    add_blocks(out_ref, own_cols, counts_ref[tile], crossed.at[0], 1 - depth)


def place_halo_kernel(counts_ref, keep_cols, swap_cols, keep, swap_in, so_far, out_ref):
    depth, tile = lax.axis_index("depth"), lax.axis_index("tile")
    last = counts_ref.shape[0] - 1

    def filled(at):
        return jnp.where((at >= 0) & (at <= last), counts_ref[jnp.clip(at, 0, last)], 0)

    by = 1 - 2 * depth
    out_ref[...] = so_far[...]
    add_blocks(out_ref, keep_cols, filled(tile - by), keep.at[0], depth)
    add_blocks(out_ref, keep_cols, filled(tile - by), keep.at[1], 1 - depth)
    add_blocks(out_ref, swap_cols, filled(tile + by), swap_in.at[0], 1 - depth)
    add_blocks(out_ref, swap_cols, filled(tile + by), swap_in.at[1], depth)


def call(kernel, in_specs, out_shapes, args, scratch=(), cost=(1 << 20, 1 << 20), aliases=None, limit=16):
    single = not isinstance(out_shapes, (list, tuple))
    return pl.pallas_call(
        kernel,
        out_shape=out_shapes if single else tuple(out_shapes),
        in_specs=in_specs,
        out_specs=VMEM if single else tuple(VMEM for _ in out_shapes),
        scratch_shapes=list(scratch),
        input_output_aliases=aliases or {},
        cost_estimate=pl.CostEstimate(flops=cost[0], bytes_accessed=cost[1], transcendentals=0),
        compiler_params=pltpu.CompilerParams(vmem_limit_bytes=limit << 20),
    )(*args)


def work(transmission, probe, scan_rows, scan_cols, tile_counts, diffraction):
    parts, per, strip, _ = transmission.shape
    size = probe.shape[-1]
    half = size // 2
    slots = scan_rows.shape[0]
    n_depth, n_tile = lax.axis_size("depth"), lax.axis_size("tile")
    slices = n_depth * per
    items = slots // n_depth

    swaps = [(d * n_tile + t, (1 - d) * n_tile + t) for d in range(n_depth) for t in range(n_tile)]
    moves = [(t, t + 1) for t in range(n_tile - 1)] + [(n_tile + t + 1, n_tile + t) for t in range(n_tile - 1)]
    asks = [(b, a) for a, b in moves]

    def send(value, pairs):
        return lax.ppermute(value, AXES, pairs)

    swap_cols = send(scan_cols, asks)
    theirs = send(transmission, swaps)
    bank = jax.ShapeDtypeStruct((items, parts, slices, strip, size), F32)
    piece = jax.ShapeDtypeStruct((items, parts, per, strip, size), F32)
    own_mine = call(cut_mine_kernel, [SMEM, VMEM], piece, (scan_cols, transmission))
    halos = []
    for across in (True, False):
        cut = call(
            functools.partial(cut_kernel, across),
            [SMEM, VMEM, VMEM],
            bank,
            (swap_cols, transmission, theirs),
        )
        halos.append(send(cut, moves))
    passed, halo_keep = halos
    halo_swap = send(passed, swaps)
    keep_cols = send(swap_cols, swaps)
    own_theirs = call(cut_mine_kernel, [SMEM, VMEM], piece, (scan_cols, theirs))

    both = jax.ShapeDtypeStruct((n_depth, items, parts, per, half, size), F32)
    crossing = jax.ShapeDtypeStruct((3, items, parts, per, half, size), F32)
    results = call(
        compute_kernel,
        [SMEM, SMEM] + [VMEM] * 8,
        [piece, both, both, crossing] + [jax.ShapeDtypeStruct((parts, half, size), F32)] * 2,
        (tile_counts, scan_rows, own_mine, own_theirs, halo_keep, halo_swap, probe, diffraction)
        + tuple(jnp.asarray(v) for v in tables(size)),
        scratch=[
            pltpu.VMEM((slices, 2 * half + strip, size), F32),
            pltpu.VMEM((slices, 2 * half + strip, size), F32),
            pltpu.VMEM((items // 2, slices, 2 * size, 2 * size), F32),
            pltpu.VMEM((items // 2, slices, 2 * size, 2 * size), F32),
            pltpu.VMEM((items // 2, 2 * size, 2 * size), F32),
            pltpu.VMEM((size, size), F32),
        ],
        cost=(6 << 30, 8 << 20),
        limit=24,
    )
    g_own, g_pass, g_keep, g_cross, p_same, p_other = results

    total = p_same + send(p_other, swaps)
    crossed = send(g_cross, swaps)
    for mask in masks_of(n_tile):
        pairs = [(d * n_tile + t, d * n_tile + (t ^ mask)) for d in range(n_depth) for t in range(n_tile)]
        total = total + lax.ppermute(total, AXES, pairs)
    g_pass = lax.dynamic_update_slice(g_pass, crossed[1:2], (1, 0, 0, 0, 0, 0))
    g_keep = lax.dynamic_update_slice(g_keep, crossed[2:3], (1, 0, 0, 0, 0, 0))
    arrived = send(g_pass, moves)
    keep = send(g_keep, moves)
    swap_in = send(arrived, swaps)

    grad_shape = jax.ShapeDtypeStruct(transmission.shape, F32)
    grad = call(
        place_own_kernel,
        [SMEM] * 2 + [VMEM] * 2,
        grad_shape,
        (tile_counts, scan_cols, g_own, crossed),
    )
    grad = call(
        place_halo_kernel,
        [SMEM] * 3 + [VMEM] * 3,
        grad_shape,
        (tile_counts, keep_cols, swap_cols, keep, swap_in, grad),
    )
    return (grad, total)


def solution(mesh):
    placed = (P(None, "depth", "tile", None), P(), P("tile"), P("tile"), P(), P("tile", None, None))
    return jax.shard_map(
        work,
        mesh=mesh,
        in_specs=placed,
        out_specs=(P(None, "depth", "tile", None), P(None, "depth", None)),
        check_vma=False,
    )
```
